256 devices in a mesh: row: 32 (over x, y, core), col: 8 (over z).
Axes of the slice: x: 4, y: 4, z: 8, core: 2. Of those that a mesh axis runs over, the one named last changes fastest.
Arguments:
- features: bfloat16 [65536, 512], P(('row', 'col')), may hold values from -6 to 6
- tile_values: bfloat16 [512, 8, 128, 4, 128], P('row', 'col'), may hold values from -0.09375 to 0.09375
- slot_refs: int32 [512, 8, 4], P('row', 'col'), may hold values from 0 to 31, as said below
- wanted: int32 [32, 8, 32, 1], P('row', 'col'), may hold values from 0 to 1, as said below
- time_ids: int32 [65536], P(('row', 'col')), may hold values from 0 to 127
- cond_ids: int32 [65536], P(('row', 'col')), may hold values from 0 to 15
- time_table: bfloat16 [128, 512], replicated, may hold values from -3 to 3
- cond_table: bfloat16 [16, 512], replicated, may hold values from -2.5 to 2.5
- gains: float32 [2, 512], replicated, may hold values from 0.1 to 1.9
- w_in: bfloat16 [2, 512, 2048], replicated, may hold values from -0.25 to 0.25
- w_out: bfloat16 [2, 2048, 512], replicated, may hold values from -0.125 to 0.125
Outputs:
- denoised: bfloat16 [65536, 512], P(('row', 'col'))
The draws below stay inside these ranges and needn't reach their ends.
Inputs may be any that keep to these rules, and one draw needn't show every extreme that they name: `slot_refs`: every value 0 to 31 is named by some slot among the rows of one device and one column block. `wanted`: the 1 offsets of one device for one peer are distinct.
All inputs are finite; a program needn't handle non-finite values.
Results may differ from the reference program's by a relative error of at most 0.006.
Values may be sent and summed in bfloat16 or wider, within the bound.
No kernel may reach another device: no remote copies, remote signals or barrier semaphores. Data moves between devices by JAX's collectives and lax.ppermute only.
A program may use at most 64 MiB of HBM per device.

```python
import jax
import jax.numpy as jnp
from jax import lax

F = 512
HID = 2048
TILE = 128
TPC = 2
SLOTS = 4
REF = 1
LAYERS = 2
TSTEPS = 128
NCOND = 16
NODES = 65536
ROWTILES = 512
SUMMED = 4096
N_ROW = 32
N_COL = 8


def draw_slot_refs(key, part):
    ref_total = N_ROW * REF
    block_size = TPC * N_COL * SLOTS
    key_list = jax.random.split(key, N_ROW * N_COL)

    def one_block(one_key):
        first_key, second_key = jax.random.split(one_key)
        extra = jax.random.randint(first_key, (block_size - ref_total,), 0, ref_total, dtype=jnp.int32)
        pool_values = jnp.concatenate([jnp.arange(ref_total, dtype=jnp.int32), extra])
        return jax.random.permutation(second_key, pool_values)
    blocks = jax.vmap(one_block)(key_list)
    blocks = blocks.reshape(N_ROW, N_COL, TPC * N_COL, SLOTS)
    return blocks.transpose(0, 2, 1, 3).reshape(N_ROW * TPC * N_COL, N_COL, SLOTS).astype(jnp.int32)


def draw_wanted(key, part):
    key_list = jax.random.split(key, N_ROW * N_COL * N_ROW)

    def offsets(one_key):
        return jax.random.permutation(one_key, TPC)[:REF].astype(jnp.int32)
    return jax.vmap(offsets)(key_list).reshape(N_ROW, N_COL, N_ROW, REF)


def touch_ends(entries, own_key, low, top_value):
    extent = entries.shape
    spot = [jax.random.randint(jax.random.fold_in(own_key, axis), (), 0, extent[axis]) for axis in range(len(extent))]
    entries = entries.at[tuple(spot)].set(low)
    longest = extent.index(max(extent))
    spot[longest] = (spot[longest] + 1) % extent[longest]
    return entries.at[tuple(spot)].set(top_value)


def shard_levels(key, dims, pieces, low, top_value):
    factor_of = 1.0
    for axis_at, parts in pieces:
        steps = jax.random.uniform(jax.random.fold_in(jax.random.fold_in(key, 6), axis_at), (parts,), jnp.float32, low / len(pieces), top_value / len(pieces))
        factor_of = factor_of * jnp.repeat(jnp.exp(steps), dims[axis_at] // parts).reshape((-1,) + (1,) * (len(dims) - 1 - axis_at))
    return factor_of


def scatter_about(key, extent, width, bound, cuts=(), kind=jnp.bfloat16):
    factor_of = shard_levels(key, extent, cuts, -0.22, 0.18) if cuts else 1.0
    result = jax.random.normal(key, extent, jnp.float32) * width * factor_of
    return jnp.minimum(jnp.maximum(result, -bound), bound).astype(kind)


def setup_inputs(seed: int = 0) -> dict:
    splits = jax.random.split(jax.random.key(seed), 12)
    features = scatter_about(splits[0], (NODES, F), 1.0, 6.0, ((0, 256),))
    tile_values = scatter_about(splits[1], (ROWTILES, N_COL, TILE, SLOTS, TILE), (SUMMED ** -0.5), 0.09375, ((0, 32), (1, 8)))
    slot_refs = draw_slot_refs(jax.random.fold_in(splits[11], 71), 0)
    wanted = draw_wanted(jax.random.fold_in(splits[11], 71), 0)
    time_ids = touch_ends(jax.random.randint(splits[4], (NODES,), 0, TSTEPS), jax.random.fold_in(splits[4], 1), 0, TSTEPS - 1).astype(jnp.int32)
    cond_ids = touch_ends(jax.random.randint(splits[5], (NODES,), 0, NCOND), jax.random.fold_in(splits[5], 1), 0, NCOND - 1).astype(jnp.int32)
    time_table = scatter_about(splits[6], (TSTEPS, F), 0.5, 3.0)
    cond_table = scatter_about(splits[7], (NCOND, F), 0.4, 2.5)
    gains = jnp.clip(1.0 + 0.18 * jax.random.normal(splits[8], (LAYERS, F), jnp.float32), 0.1, 1.9)
    w_in = scatter_about(splits[9], (LAYERS, F, HID), F ** -0.5, 0.25)
    w_out = scatter_about(splits[10], (LAYERS, HID, F), HID ** -0.5, 0.125)
    return dict(features=features, tile_values=tile_values, slot_refs=slot_refs, wanted=wanted, time_ids=time_ids, cond_ids=cond_ids, time_table=time_table, cond_table=cond_table, gains=gains, w_in=w_in, w_out=w_out)


epsilon = 1e-06

def reference(features, tile_values, slot_refs, wanted, time_ids, cond_ids, time_table, cond_table, gains, w_in, w_out):
    row_dev = (jnp.arange(ROWTILES, dtype=jnp.int32) // (TPC * N_COL))[:, None, None]
    col_dev = jnp.arange(N_COL, dtype=jnp.int32)[None, :, None]
    peer = slot_refs // REF
    which = slot_refs % REF
    offset = wanted[row_dev, col_dev, peer, which]
    col_tile = ((peer * N_COL + col_dev) * TPC + offset).astype(jnp.int32)
    cond_rows = cond_table[cond_ids].astype(jnp.float32)
    time_rows = time_table[time_ids].astype(jnp.float32)
    state = features
    for layer in range(LAYERS):
        state_tiles = state.reshape(NODES // TILE, TILE, F)

        def one_row(items):
            block, tile_ids = items
            left = block.transpose(1, 0, 2, 3).reshape(TILE, N_COL * SLOTS * TILE)
            right = state_tiles[tile_ids.reshape(-1)].reshape(N_COL * SLOTS * TILE, F)
            return jnp.dot(left, right, preferred_element_type=jnp.float32)
        aggregate = lax.map(one_row, (tile_values, col_tile)).reshape(NODES, F)
        pre = state.astype(jnp.float32) + aggregate
        scale = lax.rsqrt(lax.optimization_barrier(jnp.mean(pre * pre, axis=-1, keepdims=True)) + epsilon)
        normed = (pre * scale * gains[layer] * (1.0 + cond_rows) + time_rows).astype(jnp.bfloat16)
        inner = jnp.dot(normed, w_in[layer], preferred_element_type=jnp.float32)
        hidden = jax.nn.silu(inner).astype(jnp.bfloat16)
        state = (pre + jnp.dot(hidden, w_out[layer], preferred_element_type=jnp.float32)).astype(jnp.bfloat16)
    return state
```

```python
import jax
import jax.numpy as jnp
from jax import lax
from jax.experimental import pallas as pl
from jax.experimental.pallas import tpu as pltpu
from jax.sharding import PartitionSpec as P

LAYERS = 2
VMEM_LIMIT = 40 * 1024 * 1024

epsilon = 1e-06


def lookup(ids, table):
    onehot = (ids[:, None] == jnp.arange(table.shape[0], dtype=jnp.int32)[None, :]).astype(
        jnp.bfloat16
    )
    return jnp.dot(onehot, table, preferred_element_type=jnp.float32)


def aggregate_tiles(matrix, sources, source_row, source_slot, slot_index, order, split):
    row_tiles, tile, depth = matrix.shape
    slots = depth // tile
    width = sources[0].shape[-1]
    gathered = source_row.shape[0]
    blocks = order.shape[0]
    per_block = row_tiles // blocks
    n_src = len(sources)
    n_out = blocks if split else 1
    rows = per_block * tile

    def body(row_ref, slot_ref, index_ref, order_ref, matrix_ref, *refs):
        src = refs[:n_src]
        outs = refs[n_src : n_src + n_out]
        tiles, left, result, tile_sem, left_sem, out_sem = refs[n_src + n_out :]

        def tile_copy(b):
            start = pl.multiple_of(row_ref[b], tile)
            return pltpu.make_async_copy(
                src[b % n_src].at[pl.ds(start, tile)], tiles.at[slot_ref[b]], tile_sem.at[b]
            )

        def left_copy(k):
            return pltpu.make_async_copy(
                matrix_ref.at[pl.ds(order_ref[k] * per_block, per_block)], left.at[k], left_sem.at[k]
            )

        def out_copy(k):
            target = outs[k] if split else outs[0].at[pl.ds(k * rows, rows)]
            return pltpu.make_async_copy(result.at[k], target, out_sem.at[k])

        left_copy(0).start()
        for b in range(gathered):
            tile_copy(b).start()
        for k in range(1, blocks):
            left_copy(k).start()
        for b in range(gathered):
            tile_copy(b).wait()
        for k in range(blocks):
            left_copy(k).wait()
            for j in range(per_block):
                first = (order_ref[k] * per_block + j) * slots
                right = jnp.concatenate([tiles[index_ref[first + s]] for s in range(slots)], axis=0)
                value = jnp.dot(left[k, j], right, preferred_element_type=jnp.float32)
                result[k, j * tile : (j + 1) * tile, :] = value.astype(result.dtype)
            out_copy(k).start()
        for k in range(blocks):
            out_copy(k).wait()

    smem = pl.BlockSpec(memory_space=pltpu.SMEM)
    hbm = pl.BlockSpec(memory_space=pl.ANY)
    return pl.pallas_call(
        body,
        in_specs=[smem] * 4 + [hbm] * (1 + n_src),
        out_specs=[hbm] * n_out,
        out_shape=[jax.ShapeDtypeStruct((blocks * rows // n_out, width), jnp.bfloat16)] * n_out,
        scratch_shapes=[
            pltpu.VMEM((gathered, tile, width), jnp.bfloat16),
            pltpu.VMEM((blocks, per_block, tile, depth), jnp.bfloat16),
            pltpu.VMEM((blocks, rows, width), jnp.bfloat16),
            pltpu.SemaphoreType.DMA((gathered,)),
            pltpu.SemaphoreType.DMA((blocks,)),
            pltpu.SemaphoreType.DMA((blocks,)),
        ],
        compiler_params=pltpu.CompilerParams(vmem_limit_bytes=VMEM_LIMIT),
        name="aggregate_tiles",
    )(source_row, source_slot, slot_index, order, matrix, *sources)


def node_mlp(layer, state, parts, scale_rows, shift_rows, w_in, w_out):
    rows, width = state.shape
    hidden_units = w_in.shape[-1]
    chunks = 4
    chunk = hidden_units // chunks
    n_parts = len(parts)

    def body(state_ref, scale_ref, shift_ref, *refs):
        part_refs = refs[:n_parts]
        w_in_ref, w_out_ref, out_ref, up, down, up_sem, down_sem = refs[n_parts:]

        def up_copy(k):
            return pltpu.make_async_copy(
                w_in_ref.at[layer, :, pl.ds(k * chunk, chunk)], up.at[k], up_sem.at[k]
            )

        def down_copy(k):
            return pltpu.make_async_copy(
                w_out_ref.at[layer, pl.ds(k * chunk, chunk)], down.at[k], down_sem.at[k]
            )

        for k in range(chunks):
            up_copy(k).start()
            down_copy(k).start()
        pre = state_ref[...].astype(jnp.float32)
        for part in part_refs:
            pre = pre + part[...].astype(jnp.float32)
        scale = lax.rsqrt(jnp.mean(pre * pre, axis=-1, keepdims=True) + epsilon)
        normed = (pre * scale * scale_ref[...] + shift_ref[...].astype(jnp.float32)).astype(
            jnp.bfloat16
        )
        total = pre
        for k in range(chunks):
            up_copy(k).wait()
            inner = jnp.dot(normed, up[k], preferred_element_type=jnp.float32)
            hidden = (inner / (1.0 + jnp.exp(-inner))).astype(jnp.bfloat16)
            down_copy(k).wait()
            total = total + jnp.dot(hidden, down[k], preferred_element_type=jnp.float32)
        out_ref[...] = total.astype(out_ref.dtype)

    vmem = pl.BlockSpec(memory_space=pltpu.VMEM)
    hbm = pl.BlockSpec(memory_space=pl.ANY)
    return pl.pallas_call(
        body,
        in_specs=[vmem] * (3 + n_parts) + [hbm] * 2,
        out_specs=vmem,
        out_shape=jax.ShapeDtypeStruct((rows, width), jnp.bfloat16),
        scratch_shapes=[
            pltpu.VMEM((chunks, width, chunk), jnp.bfloat16),
            pltpu.VMEM((chunks, chunk, width), jnp.bfloat16),
            pltpu.SemaphoreType.DMA((chunks,)),
            pltpu.SemaphoreType.DMA((chunks,)),
        ],
        compiler_params=pltpu.CompilerParams(vmem_limit_bytes=VMEM_LIMIT),
        name="node_mlp",
    )(state, scale_rows, shift_rows, *parts, w_in, w_out)


def local(
    features,
    tile_values,
    slot_refs,
    wanted,
    time_ids,
    cond_ids,
    time_table,
    cond_table,
    gains,
    w_in,
    w_out,
):
    row_count = lax.axis_size("row")
    col_count = lax.axis_size("col")
    span, width = features.shape
    tile = tile_values.shape[-1]
    slots = tile_values.shape[3]
    row_tiles = tile_values.shape[0]
    refer = wanted.shape[-1]
    matrix = tile_values.reshape(row_tiles, tile, slots * tile)
    slot_index = slot_refs.reshape(-1)
    peers = jnp.arange(row_count, dtype=jnp.int32)[:, None]
    source_row = (peers * span + wanted.reshape(row_count, refer) * tile).reshape(-1)
    source_slot = jnp.arange(row_count * refer, dtype=jnp.int32)
    order = jnp.arange(col_count, dtype=jnp.int32)
    scale_rows = gains[:, None, :] * (1.0 + lookup(cond_ids, cond_table))[None]
    shift_rows = lookup(time_ids, time_table).astype(jnp.bfloat16)
    state = features
    for layer in range(LAYERS):
        column = lax.all_gather(state, "row", axis=0, tiled=True)
        (product,) = aggregate_tiles(matrix, [column], source_row, source_slot, slot_index, order, False)
        aggregate = lax.psum_scatter(product, "col", scatter_dimension=0, tiled=True)
        state = node_mlp(layer, state, [aggregate], scale_rows[layer], shift_rows, w_in, w_out)
    return state


def solution(mesh):
    return jax.shard_map(
        local,
        mesh=mesh,
        in_specs=(
            P(("row", "col"), None),
            P("row", "col", None, None, None),
            P("row", "col", None),
            P("row", "col", None, None),
            P(("row", "col")),
            P(("row", "col")),
            P(),
            P(),
            P(),
            P(),
            P(),
        ),
        out_specs=P(("row", "col"), None),
        check_vma=False,
    )
```

```python
import jax
import jax.numpy as jnp
from jax import lax
from jax.experimental import pallas as pl
from jax.experimental.pallas import tpu as pltpu
from jax.sharding import PartitionSpec as P

LAYERS = 2
VMEM_LIMIT = 40 * 1024 * 1024

epsilon = 1e-06


def lookup(ids, table):
    onehot = (ids[:, None] == jnp.arange(table.shape[0], dtype=jnp.int32)[None, :]).astype(
        jnp.bfloat16
    )
    return jnp.dot(onehot, table, preferred_element_type=jnp.float32)


def aggregate_tiles(
    matrix, sources, source_of, source_row, source_slot, slot_index, order, split
):
    row_tiles, tile, depth = matrix.shape
    slots = depth // tile
    width = sources[0].shape[-1]
    gathered = source_row.shape[0]
    blocks = order.shape[0]
    per_block = row_tiles // blocks
    n_src = len(sources)
    n_out = blocks if split else 1
    rows = per_block * tile

    def body(row_ref, slot_ref, index_ref, order_ref, matrix_ref, *refs):
        src = refs[:n_src]
        outs = refs[n_src : n_src + n_out]
        tiles, left, result, tile_sem, left_sem, out_sem = refs[n_src + n_out :]

        def tile_copy(b):
            start = pl.multiple_of(row_ref[b], tile)
            return pltpu.make_async_copy(
                src[source_of[b]].at[pl.ds(start, tile)], tiles.at[slot_ref[b]], tile_sem.at[b]
            )

        def left_copy(k):
            return pltpu.make_async_copy(
                matrix_ref.at[pl.ds(order_ref[k] * per_block, per_block)], left.at[k], left_sem.at[k]
            )

        def out_copy(k):
            target = outs[k] if split else outs[0].at[pl.ds(k * rows, rows)]
            return pltpu.make_async_copy(result.at[k], target, out_sem.at[k])

        left_copy(0).start()
        for b in range(gathered):
            tile_copy(b).start()
        for k in range(1, blocks):
            left_copy(k).start()
        for b in range(gathered):
            tile_copy(b).wait()
        for k in range(blocks):
            left_copy(k).wait()
            for j in range(per_block):
                first = (order_ref[k] * per_block + j) * slots
                right = jnp.concatenate([tiles[index_ref[first + s]] for s in range(slots)], axis=0)
                value = jnp.dot(left[k, j], right, preferred_element_type=jnp.float32)
                result[k, j * tile : (j + 1) * tile, :] = value.astype(result.dtype)
            out_copy(k).start()
        for k in range(blocks):
            out_copy(k).wait()

    smem = pl.BlockSpec(memory_space=pltpu.SMEM)
    hbm = pl.BlockSpec(memory_space=pltpu.HBM)
    return pl.pallas_call(
        body,
        in_specs=[smem] * 4 + [hbm] * (1 + n_src),
        out_specs=[hbm] * n_out,
        out_shape=[jax.ShapeDtypeStruct((blocks * rows // n_out, width), jnp.bfloat16)] * n_out,
        scratch_shapes=[
            pltpu.VMEM((gathered, tile, width), jnp.bfloat16),
            pltpu.VMEM((blocks, per_block, tile, depth), jnp.bfloat16),
            pltpu.VMEM((blocks, rows, width), jnp.bfloat16),
            pltpu.SemaphoreType.DMA((gathered,)),
            pltpu.SemaphoreType.DMA((blocks,)),
            pltpu.SemaphoreType.DMA((blocks,)),
        ],
        compiler_params=pltpu.CompilerParams(vmem_limit_bytes=VMEM_LIMIT),
        name="aggregate_tiles",
    )(source_row, source_slot, slot_index, order, matrix, *sources)


def node_mlp(layer, state, parts, scale_rows, shift_rows, w_in, w_out):
    rows, width = state.shape
    hidden_units = w_in.shape[-1]
    chunks = 4
    chunk = hidden_units // chunks
    n_parts = len(parts)

    def body(state_ref, scale_ref, shift_ref, *refs):
        part_refs = refs[:n_parts]
        w_in_ref, w_out_ref, out_ref, up, down, up_sem, down_sem = refs[n_parts:]

        def up_copy(k):
            return pltpu.make_async_copy(
                w_in_ref.at[layer, :, pl.ds(k * chunk, chunk)], up.at[k], up_sem.at[k]
            )

        def down_copy(k):
            return pltpu.make_async_copy(
                w_out_ref.at[layer, pl.ds(k * chunk, chunk)], down.at[k], down_sem.at[k]
            )

        for k in range(chunks):
            up_copy(k).start()
            down_copy(k).start()
        pre = state_ref[...].astype(jnp.float32)
        for part in part_refs:
            pre = pre + part[...].astype(jnp.float32)
        scale = lax.rsqrt(jnp.mean(pre * pre, axis=-1, keepdims=True) + epsilon)
        normed = (pre * scale * scale_ref[...] + shift_ref[...].astype(jnp.float32)).astype(
            jnp.bfloat16
        )
        total = pre
        for k in range(chunks):
            up_copy(k).wait()
            inner = jnp.dot(normed, up[k], preferred_element_type=jnp.float32)
            hidden = (inner / (1.0 + jnp.exp(-inner))).astype(jnp.bfloat16)
            down_copy(k).wait()
            total = total + jnp.dot(hidden, down[k], preferred_element_type=jnp.float32)
        out_ref[...] = total.astype(out_ref.dtype)

    vmem = pl.BlockSpec(memory_space=pltpu.VMEM)
    hbm = pl.BlockSpec(memory_space=pltpu.HBM)
    return pl.pallas_call(
        body,
        in_specs=[vmem] * (3 + n_parts) + [hbm] * 2,
        out_specs=vmem,
        out_shape=jax.ShapeDtypeStruct((rows, width), jnp.bfloat16),
        scratch_shapes=[
            pltpu.VMEM((chunks, width, chunk), jnp.bfloat16),
            pltpu.VMEM((chunks, chunk, width), jnp.bfloat16),
            pltpu.SemaphoreType.DMA((chunks,)),
            pltpu.SemaphoreType.DMA((chunks,)),
        ],
        compiler_params=pltpu.CompilerParams(vmem_limit_bytes=VMEM_LIMIT),
        name="node_mlp",
    )(state, scale_rows, shift_rows, *parts, w_in, w_out)


SIDE = 4
NEAR = (1, -1, 2)


def place(x, y, core):
    return ((x % SIDE) * SIDE + y % SIDE) * 2 + core


def pull(value, first, distance):
    pairs = []
    for x in range(SIDE):
        for y in range(SIDE):
            for core in range(2):
                step = (distance, 0) if (core == 0) == first else (0, distance)
                pairs.append((place(x + step[0], y + step[1], core), place(x, y, core)))
    return lax.ppermute(value, "row", pairs)


def swap(value):
    count = 2 * SIDE * SIDE
    return lax.ppermute(value, "row", [(i, i ^ 1) for i in range(count)])


def gather_blocks(own):
    rows = own.shape[0]
    line = [pull(own, True, e) for e in NEAR]
    across = [pull(own, False, d) for d in NEAR]
    lines = jnp.concatenate(line, axis=0)
    far = [pull(lines, False, d) for d in NEAR]
    arrays = [own, lines] + across + far
    offsets = [[(0, 0)], [(e, 0) for e in NEAR]]
    offsets += [[(0, d)] for d in NEAR]
    offsets += [[(e, d) for e in NEAR] for d in NEAR]
    blocks = []
    count = len(arrays)
    for swapped in (0, 1):
        for a, held in enumerate(offsets):
            for k, (e, d) in enumerate(held):
                blocks.append((a + swapped * count, k * rows, e, d, swapped))
    return arrays + [swap(v) for v in arrays], blocks


def send(value, distance):
    count = lax.axis_size("col")
    return lax.ppermute(value, "col", [(i, (i + distance) % count) for i in range(count)])


def sum_columns(near, own):
    half = own.shape[0] // 2
    far_up = send(near[4][:half], 2)
    far_down = send(near[4][half:], -2)
    up = send(near[3], 1)
    down = send(near[5], -1)
    next_up = send(near[1], 1)
    next_down = send(near[7], -1)
    f32 = jnp.float32
    relay_up = near[2].astype(f32) + up.astype(f32)
    relay_up = jnp.concatenate([relay_up[:half] + far_up.astype(f32), relay_up[half:]], axis=0)
    relay_down = near[6].astype(f32) + down.astype(f32)
    relay_down = jnp.concatenate(
        [relay_down[:half], relay_down[half:] + far_down.astype(f32)], axis=0
    )
    last_up = send(relay_up.astype(jnp.bfloat16), 2)
    last_down = send(relay_down.astype(jnp.bfloat16), -2)
    return [own, next_up, next_down, last_up, last_down]


def local(
    features,
    tile_values,
    slot_refs,
    wanted,
    time_ids,
    cond_ids,
    time_table,
    cond_table,
    gains,
    w_in,
    w_out,
):
    col_count = lax.axis_size("col")
    tile = tile_values.shape[-1]
    slots = tile_values.shape[3]
    row_tiles = tile_values.shape[0]
    matrix = tile_values.reshape(row_tiles, tile, slots * tile)
    slot_index = slot_refs.reshape(-1)
    row = lax.axis_index("row")
    x, y, core = row // (2 * SIDE), row // 2 % SIDE, row % 2
    order = (lax.axis_index("col") + jnp.arange(col_count, dtype=jnp.int32)) % col_count
    scale_rows = gains[:, None, :] * (1.0 + lookup(cond_ids, cond_table))[None]
    shift_rows = lookup(time_ids, time_table).astype(jnp.bfloat16)
    state = features
    for layer in range(LAYERS):
        arrays, blocks = gather_blocks(state)
        table = jnp.array(blocks, dtype=jnp.int32)
        base, first, second, held = table[:, 1], table[:, 2], table[:, 3], core ^ table[:, 4]
        source_slot = jnp.where(
            held == 0, place(x + first, y + second, 0), place(x + second, y + first, 1)
        )
        source_row = base + wanted.reshape(-1)[source_slot] * tile
        near = aggregate_tiles(
            matrix,
            arrays,
            [b[0] for b in blocks],
            source_row,
            source_slot,
            slot_index,
            order,
            True,
        )
        parts = sum_columns(near, near[0])
        state = node_mlp(layer, state, parts, scale_rows[layer], shift_rows, w_in, w_out)
    return state


def solution(mesh):
    return jax.shard_map(
        local,
        mesh=mesh,
        in_specs=(
            P(("row", "col"), None),
            P("row", "col", None, None, None),
            P("row", "col", None),
            P("row", "col", None, None),
            P(("row", "col")),
            P(("row", "col")),
            P(),
            P(),
            P(),
            P(),
            P(),
        ),
        out_specs=P(("row", "col"), None),
        check_vma=False,
    )
```

```python
import jax
import jax.numpy as jnp
from jax import lax
from jax.experimental import pallas as pl
from jax.experimental.pallas import tpu as pltpu
from jax.sharding import PartitionSpec as P

LAYERS = 2
PIECES = 1
VMEM_LIMIT = 22 * 1024 * 1024

epsilon = 1e-06


def lookup(ids, table):
    onehot = (ids[:, None] == jnp.arange(table.shape[0], dtype=jnp.int32)[None, :]).astype(
        jnp.bfloat16
    )
    return jnp.dot(onehot, table, preferred_element_type=jnp.float32)


def aggregate_tiles(matrix, sources, source_of, source_row, source_slot, slot_index, order):
    row_tiles, tile, depth = matrix.shape
    slots = depth // tile
    width = sources[0].shape[-1]
    gathered = source_row.shape[0]
    blocks = order.shape[0]
    per_block = row_tiles // blocks
    n_src = len(sources)
    rows = per_block * tile

    def body(row_ref, slot_ref, index_ref, order_ref, matrix_ref, *refs):
        src = refs[:n_src]
        outs = refs[n_src : n_src + blocks]
        (tiles,) = refs[n_src + blocks :]
        for b in range(gathered):
            start = pl.multiple_of(row_ref[b], tile)
            tiles[slot_ref[b]] = src[source_of[b]][pl.ds(start, tile), :]
        for k in range(blocks):
            for j in range(per_block):
                t = order_ref[k] * per_block + j
                right = jnp.concatenate(
                    [tiles[index_ref[t * slots + s]] for s in range(slots)], axis=0
                )
                value = jnp.dot(matrix_ref[t], right, preferred_element_type=jnp.float32)
                outs[k][j * tile : (j + 1) * tile, :] = value.astype(jnp.bfloat16)

    smem = pl.BlockSpec(memory_space=pltpu.SMEM)
    vmem = pl.BlockSpec(memory_space=pltpu.VMEM)
    return pl.pallas_call(
        body,
        in_specs=[smem] * 4 + [vmem] * (1 + n_src),
        out_specs=[vmem] * blocks,
        out_shape=[jax.ShapeDtypeStruct((rows, width), jnp.bfloat16)] * blocks,
        scratch_shapes=[pltpu.VMEM((gathered, tile, width), jnp.bfloat16)],
        compiler_params=pltpu.CompilerParams(vmem_limit_bytes=VMEM_LIMIT),
        name="aggregate_tiles",
    )(source_row, source_slot, slot_index, order, matrix, *sources)


def node_mlp(layer, states, parts, scale_rows, shift_rows, w_in, w_out, pieces):
    rows = states[0].shape[0]
    width = w_out.shape[-1]
    hidden_units = w_in.shape[-1]
    chunks = 4
    chunk = hidden_units // chunks
    given = [[state, *addends] for state, addends in zip(states, parts, strict=True)]
    flat = [value for group in given for value in group]

    def body(scale_ref, shift_ref, w_in_ref, w_out_ref, *refs):
        inputs, outs = list(refs[: len(flat)]), refs[len(flat) :]
        sums = []
        for group in given:
            total = inputs.pop(0)[...].astype(jnp.float32)
            for _ in group[1:]:
                total = total + inputs.pop(0)[...].astype(jnp.float32)
            sums.append(total)
        pre = jnp.concatenate(sums, axis=1)
        scale = lax.rsqrt(jnp.mean(pre * pre, axis=-1, keepdims=True) + epsilon)
        normed = (
            pre * scale * scale_ref[layer] + shift_ref[...].astype(jnp.float32)
        ).astype(jnp.bfloat16)
        total = pre
        for k in range(chunks):
            units = pl.ds(k * chunk, chunk)
            inner = jnp.dot(
                normed, w_in_ref[layer, :, units], preferred_element_type=jnp.float32
            )
            hidden = (0.5 * inner * (1.0 + jnp.tanh(0.5 * inner))).astype(jnp.bfloat16)
            total = total + jnp.dot(
                hidden, w_out_ref[layer, units, :], preferred_element_type=jnp.float32
            )
        piece = width // pieces
        for p in range(pieces):
            outs[p][...] = total[:, p * piece : (p + 1) * piece].astype(jnp.bfloat16)

    vmem = pl.BlockSpec(memory_space=pltpu.VMEM)
    return pl.pallas_call(
        body,
        in_specs=[vmem] * (4 + len(flat)),
        out_specs=[vmem] * pieces,
        out_shape=[jax.ShapeDtypeStruct((rows, width // pieces), jnp.bfloat16)] * pieces,
        compiler_params=pltpu.CompilerParams(vmem_limit_bytes=VMEM_LIMIT),
        name="node_mlp",
    )(scale_rows, shift_rows, w_in, w_out, *flat)


SIDE = 4
NEAR = (1, -1, 2)


def held_blocks():
    offsets = [[(e, d) for e in (0, *NEAR)] for d in (0, *NEAR)]
    count = len(offsets)
    return [
        (a + swapped * count, k, e, d, swapped)
        for swapped in (0, 1)
        for a, held in enumerate(offsets)
        for k, (e, d) in enumerate(held)
    ]


BLOCKS = held_blocks()


def place(x, y, core):
    return ((x % SIDE) * SIDE + y % SIDE) * 2 + core


def pull(value, first, distance):
    pairs = []
    for x in range(SIDE):
        for y in range(SIDE):
            for core in range(2):
                step = (distance, 0) if (core == 0) == first else (0, distance)
                pairs.append((place(x + step[0], y + step[1], core), place(x, y, core)))
    return lax.ppermute(value, "row", pairs)


def swap(value):
    count = 2 * SIDE * SIDE
    return lax.ppermute(value, "row", [(i, i ^ 1) for i in range(count)])


def gather_blocks(own):
    line = jnp.concatenate([own] + [pull(own, True, e) for e in NEAR], axis=0)
    arrays = [line] + [pull(line, False, d) for d in NEAR]
    return arrays + [swap(v) for v in arrays]


def send(value, distance):
    count = lax.axis_size("col")
    return lax.ppermute(value, "col", [(i, (i + distance) % count) for i in range(count)])


def sum_columns(near, own):
    half = own.shape[0] // 2
    far_up = send(near[4][:half], 2)
    far_down = send(near[4][half:], -2)
    up = send(near[3], 1)
    down = send(near[5], -1)
    next_up = send(near[1], 1)
    next_down = send(near[7], -1)
    f32 = jnp.float32
    relay_up = near[2].astype(f32) + up.astype(f32)
    relay_up = jnp.concatenate([relay_up[:half] + far_up.astype(f32), relay_up[half:]], axis=0)
    relay_down = near[6].astype(f32) + down.astype(f32)
    relay_down = jnp.concatenate(
        [relay_down[:half], relay_down[half:] + far_down.astype(f32)], axis=0
    )
    last_up = send(relay_up.astype(jnp.bfloat16), 2)
    last_down = send(relay_down.astype(jnp.bfloat16), -2)
    return [own, next_up, next_down, last_up, last_down]


def local(
    features,
    tile_values,
    slot_refs,
    wanted,
    time_ids,
    cond_ids,
    time_table,
    cond_table,
    gains,
    w_in,
    w_out,
):
    col_count = lax.axis_size("col")
    span = features.shape[0]
    tile = tile_values.shape[-1]
    slots = tile_values.shape[3]
    row_tiles = tile_values.shape[0]
    matrix = tile_values.reshape(row_tiles, tile, slots * tile)
    slot_index = slot_refs.reshape(-1)
    row = lax.axis_index("row")
    x, y, core = row // (2 * SIDE), row // 2 % SIDE, row % 2
    order = (lax.axis_index("col") + jnp.arange(col_count, dtype=jnp.int32)) % col_count
    scale_rows = gains[:, None, :] * (1.0 + lookup(cond_ids, cond_table))[None]
    shift_rows = lookup(time_ids, time_table).astype(jnp.bfloat16)
    table = jnp.array(BLOCKS, dtype=jnp.int32)
    base, first, second, held = table[:, 1] * span, table[:, 2], table[:, 3], core ^ table[:, 4]
    source_slot = jnp.where(
        held == 0, place(x + first, y + second, 0), place(x + second, y + first, 1)
    )
    source_row = base + wanted.reshape(-1)[source_slot] * tile
    piece = features.shape[1] // PIECES
    states = [features[:, p * piece : (p + 1) * piece] for p in range(PIECES)]
    for layer in range(LAYERS):
        parts = []
        for state in states:
            near = aggregate_tiles(
                matrix,
                gather_blocks(state),
                [b[0] for b in BLOCKS],
                source_row,
                source_slot,
                slot_index,
                order,
            )
            parts.append(sum_columns(near, near[0]))
        last = layer == LAYERS - 1
        states = node_mlp(
            layer,
            states,
            parts,
            scale_rows,
            shift_rows,
            w_in,
            w_out,
            1 if last else PIECES,
        )
    return states[0]


def solution(mesh):
    return jax.shard_map(
        local,
        mesh=mesh,
        in_specs=(
            P(("row", "col"), None),
            P("row", "col", None, None, None),
            P("row", "col", None),
            P("row", "col", None, None),
            P(("row", "col")),
            P(("row", "col")),
            P(),
            P(),
            P(),
            P(),
            P(),
        ),
        out_specs=P(("row", "col"), None),
        check_vma=False,
    )
```

```python
import jax
import jax.numpy as jnp
from jax import lax
from jax.experimental import pallas as pl
from jax.experimental.pallas import tpu as pltpu
from jax.sharding import PartitionSpec as P

LAYERS = 2
PIECES = 1
VMEM_LIMIT = 20 * 1024 * 1024

epsilon = 1e-06


def lookup(ids, table):
    onehot = (ids[:, None] == jnp.arange(table.shape[0], dtype=jnp.int32)[None, :]).astype(
        jnp.bfloat16
    )
    return jnp.dot(onehot, table, preferred_element_type=jnp.float32)


def aggregate_tiles(matrix, sources, here, wanted, slot_index, further):
    row_tiles, tile, depth = matrix.shape
    slots = depth // tile
    width = sources[0].shape[-1]
    count = lax.axis_size("col")
    per_block = row_tiles // count
    n_src = len(sources)
    rows = per_block * tile

    def body(here_ref, wanted_ref, index_ref, matrix_ref, *refs):
        src = refs[:n_src]
        outs = refs[n_src:-1]
        tiles = refs[-1]
        x, y, core, col = (here_ref[i] for i in range(4))
        for array, block, first, second, swapped in BLOCKS:
            held = core ^ swapped
            step_x = jnp.where(held == 0, first, second)
            step_y = jnp.where(held == 0, second, first)
            p = place(x + step_x + SIDE, y + step_y + SIDE, held)
            start = pl.multiple_of(block * rows + wanted_ref[p] * tile, tile)
            tiles[p] = src[array][pl.ds(start, tile), :]
        for out, k in zip(outs, further, strict=True):
            for j in range(per_block):
                t = (col + k) % count * per_block + j
                right = jnp.concatenate(
                    [tiles[index_ref[t * slots + s]] for s in range(slots)], axis=0
                )
                value = jnp.dot(matrix_ref[t], right, preferred_element_type=jnp.float32)
                out[j * tile : (j + 1) * tile, :] = value.astype(jnp.bfloat16)

    smem = pl.BlockSpec(memory_space=pltpu.SMEM)
    vmem = pl.BlockSpec(memory_space=pltpu.VMEM)
    return pl.pallas_call(
        body,
        in_specs=[smem] * 3 + [vmem] * (1 + n_src),
        out_specs=[vmem] * len(further),
        out_shape=[jax.ShapeDtypeStruct((rows, width), jnp.bfloat16)] * len(further),
        scratch_shapes=[pltpu.VMEM((len(BLOCKS), tile, width), jnp.bfloat16)],
        compiler_params=pltpu.CompilerParams(vmem_limit_bytes=VMEM_LIMIT),
        name="aggregate_tiles",
    )(here, wanted, slot_index, matrix, *sources)


def node_mlp(layer, states, parts, scale_rows, shift_rows, w_in, w_out, pieces):
    rows = states[0].shape[0]
    width = w_out.shape[-1]
    hidden_units = w_in.shape[-1]
    chunks = 4
    chunk = hidden_units // chunks
    given = [[state, *addends] for state, addends in zip(states, parts, strict=True)]
    flat = [value for group in given for value in group]

    def body(scale_ref, shift_ref, w_in_ref, w_out_ref, *refs):
        inputs, outs = list(refs[: len(flat)]), refs[len(flat) :]
        sums = []
        for group in given:
            total = inputs.pop(0)[...].astype(jnp.float32)
            for _ in group[1:]:
                total = total + inputs.pop(0)[...].astype(jnp.float32)
            sums.append(total)
        pre = jnp.concatenate(sums, axis=1)
        scale = lax.rsqrt(jnp.mean(pre * pre, axis=-1, keepdims=True) + epsilon)
        normed = (
            pre * scale * scale_ref[layer] + shift_ref[...].astype(jnp.float32)
        ).astype(jnp.bfloat16)
        total = pre
        for k in range(chunks):
            units = pl.ds(k * chunk, chunk)
            inner = jnp.dot(
                normed, w_in_ref[layer, :, units], preferred_element_type=jnp.float32
            )
            hidden = (0.5 * inner * (1.0 + jnp.tanh(0.5 * inner))).astype(jnp.bfloat16)
            total = total + jnp.dot(
                hidden, w_out_ref[layer, units, :], preferred_element_type=jnp.float32
            )
        piece = width // pieces
        for p in range(pieces):
            outs[p][...] = total[:, p * piece : (p + 1) * piece].astype(jnp.bfloat16)

    vmem = pl.BlockSpec(memory_space=pltpu.VMEM)
    return pl.pallas_call(
        body,
        in_specs=[vmem] * (4 + len(flat)),
        out_specs=[vmem] * pieces,
        out_shape=[jax.ShapeDtypeStruct((rows, width // pieces), jnp.bfloat16)] * pieces,
        compiler_params=pltpu.CompilerParams(vmem_limit_bytes=VMEM_LIMIT),
        name="node_mlp",
    )(scale_rows, shift_rows, w_in, w_out, *flat)


SIDE = 4
NEAR = (1, -1, 2)


def held_blocks():
    offsets = [[(e, d) for e in (0, *NEAR)] for d in (0, *NEAR)]
    count = len(offsets)
    return [
        (a + swapped * count, k, e, d, swapped)
        for swapped in (0, 1)
        for a, held in enumerate(offsets)
        for k, (e, d) in enumerate(held)
    ]


BLOCKS = held_blocks()
SENT = ((3, 5, 4), (2, 6, 1, 7, 0))


def place(x, y, core):
    return ((x % SIDE) * SIDE + y % SIDE) * 2 + core


def pull(value, first, distance):
    pairs = []
    for x in range(SIDE):
        for y in range(SIDE):
            for core in range(2):
                step = (distance, 0) if (core == 0) == first else (0, distance)
                pairs.append((place(x + step[0], y + step[1], core), place(x, y, core)))
    return lax.ppermute(value, "row", pairs)


def swap(value):
    count = 2 * SIDE * SIDE
    return lax.ppermute(value, "row", [(i, i ^ 1) for i in range(count)])


def gather_blocks(own, ready):
    after = lax.optimization_barrier
    line = jnp.concatenate([own] + [pull(own, True, e) for e in NEAR], axis=0)
    far = [pull(line, False, d) for d in NEAR]
    first = swap(line)
    far, first, ready = after((far, first, ready))
    return [line] + far + [first] + [swap(v) for v in far], ready


def send(value, distance):
    count = lax.axis_size("col")
    return lax.ppermute(value, "col", [(i, (i + distance) % count) for i in range(count)])


def sum_columns(near, own):
    half = own.shape[0] // 2
    far_up = send(near[4][:half], 2)
    far_down = send(near[4][half:], -2)
    up = send(near[3], 1)
    down = send(near[5], -1)
    next_up = send(near[1], 1)
    next_down = send(near[7], -1)
    f32 = jnp.float32
    relay_up = near[2].astype(f32) + up.astype(f32)
    relay_up = jnp.concatenate([relay_up[:half] + far_up.astype(f32), relay_up[half:]], axis=0)
    relay_down = near[6].astype(f32) + down.astype(f32)
    relay_down = jnp.concatenate(
        [relay_down[:half], relay_down[half:] + far_down.astype(f32)], axis=0
    )
    last_up = send(relay_up.astype(jnp.bfloat16), 2)
    last_down = send(relay_down.astype(jnp.bfloat16), -2)
    return [own, next_up, next_down, last_up, last_down]


def local(
    features,
    tile_values,
    slot_refs,
    wanted,
    time_ids,
    cond_ids,
    time_table,
    cond_table,
    gains,
    w_in,
    w_out,
):
    tile = tile_values.shape[-1]
    slots = tile_values.shape[3]
    row_tiles = tile_values.shape[0]
    matrix = tile_values.reshape(row_tiles, tile, slots * tile)
    slot_index = slot_refs.reshape(-1)
    wanted = wanted.reshape(-1)
    row = lax.axis_index("row")
    here = jnp.stack([row // (2 * SIDE), row // 2 % SIDE, row % 2, lax.axis_index("col")])
    scale_rows = gains[:, None, :] * (1.0 + lookup(cond_ids, cond_table))[None]
    shift_rows = lookup(time_ids, time_table).astype(jnp.bfloat16)
    piece = features.shape[1] // PIECES
    states = [features[:, p * piece : (p + 1) * piece] for p in range(PIECES)]
    ready = (matrix, wanted, slot_index, here)
    for layer in range(LAYERS):
        arrays, ready = gather_blocks(states[0], ready)
        matrix, wanted, slot_index, here = ready
        near = {}
        for group in SENT:
            products = aggregate_tiles(matrix, arrays, here, wanted, slot_index, group)
            near.update(zip(group, products, strict=True))
        parts = [sum_columns(near, near[0])]
        last = layer == LAYERS - 1
        states = node_mlp(
            layer,
            states,
            parts,
            scale_rows,
            shift_rows,
            w_in,
            w_out,
            1 if last else PIECES,
        )
    return states[0]


def solution(mesh):
    return jax.shard_map(
        local,
        mesh=mesh,
        in_specs=(
            P(("row", "col"), None),
            P("row", "col", None, None, None),
            P("row", "col", None),
            P("row", "col", None, None),
            P(("row", "col")),
            P(("row", "col")),
            P(),
            P(),
            P(),
            P(),
            P(),
        ),
        out_specs=P(("row", "col"), None),
        check_vma=False,
    )
```

```python
import jax
import jax.numpy as jnp
from jax import lax
from jax.experimental import pallas as pl
from jax.experimental.pallas import tpu as pltpu
from jax.sharding import PartitionSpec as P

LAYERS = 2
PIECES = 1
VMEM_LIMIT = 20 * 1024 * 1024

epsilon = 1e-06


def lookup(ids, table):
    onehot = (ids[:, None] == jnp.arange(table.shape[0], dtype=jnp.int32)[None, :]).astype(
        jnp.bfloat16
    )
    return jnp.dot(onehot, table, preferred_element_type=jnp.float32)


def aggregate_tiles(matrix, sources, here, wanted, slot_index, further):
    row_tiles, tile, depth = matrix.shape
    slots = depth // tile
    width = sources[0].shape[-1]
    count = lax.axis_size("col")
    per_block = row_tiles // count
    n_src = len(sources)
    rows = per_block * tile

    def body(here_ref, wanted_ref, index_ref, matrix_ref, *refs):
        src = refs[:n_src]
        outs = refs[n_src:-1]
        tiles = refs[-1]
        x, y, core, col = (here_ref[i] for i in range(4))
        for array, block, first, second, swapped in BLOCKS:
            held = core ^ swapped
            step_x = jnp.where(held == 0, first, second)
            step_y = jnp.where(held == 0, second, first)
            p = place(x + step_x + SIDE, y + step_y + SIDE, held)
            start = pl.multiple_of(block * rows + wanted_ref[p] * tile, tile)
            tiles[p] = src[array][pl.ds(start, tile), :]
        for out, k in zip(outs, further, strict=True):
            for j in range(per_block):
                t = (col + k) % count * per_block + j
                right = jnp.concatenate(
                    [tiles[index_ref[t * slots + s]] for s in range(slots)], axis=0
                )
                value = jnp.dot(matrix_ref[t], right, preferred_element_type=jnp.float32)
                out[j * tile : (j + 1) * tile, :] = value.astype(jnp.bfloat16)

    smem = pl.BlockSpec(memory_space=pltpu.SMEM)
    vmem = pl.BlockSpec(memory_space=pltpu.VMEM)
    return pl.pallas_call(
        body,
        in_specs=[smem] * 3 + [vmem] * (1 + n_src),
        out_specs=[vmem] * len(further),
        out_shape=[jax.ShapeDtypeStruct((rows, width), jnp.bfloat16)] * len(further),
        scratch_shapes=[pltpu.VMEM((len(BLOCKS), tile, width), jnp.bfloat16)],
        compiler_params=pltpu.CompilerParams(vmem_limit_bytes=VMEM_LIMIT),
        name="aggregate_tiles",
    )(here, wanted, slot_index, matrix, *sources)


def node_mlp(layer, states, parts, scale_rows, shift_rows, w_in, w_out, pieces):
    rows = states[0].shape[0]
    width = w_out.shape[-1]
    hidden_units = w_in.shape[-1]
    chunks = 4
    chunk = hidden_units // chunks
    given = [[state, *addends] for state, addends in zip(states, parts, strict=True)]
    flat = [value for group in given for value in group]

    def body(scale_ref, shift_ref, w_in_ref, w_out_ref, *refs):
        inputs, outs = list(refs[: len(flat)]), refs[len(flat) :]
        sums = []
        for group in given:
            total = inputs.pop(0)[...].astype(jnp.float32)
            for _ in group[1:]:
                total = total + inputs.pop(0)[...].astype(jnp.float32)
            sums.append(total)
        pre = jnp.concatenate(sums, axis=1)
        scale = lax.rsqrt(jnp.mean(pre * pre, axis=-1, keepdims=True) + epsilon)
        normed = (
            pre * scale * scale_ref[layer] + shift_ref[...].astype(jnp.float32)
        ).astype(jnp.bfloat16)
        total = pre
        for k in range(chunks):
            units = pl.ds(k * chunk, chunk)
            inner = jnp.dot(
                normed, w_in_ref[layer, :, units], preferred_element_type=jnp.float32
            )
            hidden = (0.5 * inner * (1.0 + jnp.tanh(0.5 * inner))).astype(jnp.bfloat16)
            total = total + jnp.dot(
                hidden, w_out_ref[layer, units, :], preferred_element_type=jnp.float32
            )
        piece = width // pieces
        for p in range(pieces):
            outs[p][...] = total[:, p * piece : (p + 1) * piece].astype(jnp.bfloat16)

    vmem = pl.BlockSpec(memory_space=pltpu.VMEM)
    return pl.pallas_call(
        body,
        in_specs=[vmem] * (4 + len(flat)),
        out_specs=[vmem] * pieces,
        out_shape=[jax.ShapeDtypeStruct((rows, width // pieces), jnp.bfloat16)] * pieces,
        compiler_params=pltpu.CompilerParams(vmem_limit_bytes=VMEM_LIMIT),
        name="node_mlp",
    )(scale_rows, shift_rows, w_in, w_out, *flat)


SIDE = 4
NEAR = (1, -1, 2)


def held_blocks():
    line = (0, *NEAR)
    offsets = [[(e, d) for e in line] for d in (0, 1, -1)]
    offsets += [[(e, 2) for e in line[:2]], [(e, 2) for e in line[2:]]]
    count = len(offsets)
    return [
        (a + swapped * count, k, e, d, swapped)
        for swapped in (0, 1)
        for a, held in enumerate(offsets)
        for k, (e, d) in enumerate(held)
    ]


BLOCKS = held_blocks()
SENT = ((3, 5, 4), (2, 6, 1, 7, 0))


def place(x, y, core):
    return ((x % SIDE) * SIDE + y % SIDE) * 2 + core


def pull(value, first, distance):
    pairs = []
    for x in range(SIDE):
        for y in range(SIDE):
            for core in range(2):
                step = (distance, 0) if (core == 0) == first else (0, distance)
                pairs.append((place(x + step[0], y + step[1], core), place(x, y, core)))
    return lax.ppermute(value, "row", pairs)


def swap(value):
    count = 2 * SIDE * SIDE
    return lax.ppermute(value, "row", [(i, i ^ 1) for i in range(count)])


def gather_blocks(own, ready):
    after = lax.optimization_barrier
    line = jnp.concatenate([own] + [pull(own, True, e) for e in NEAR], axis=0)
    half = line.shape[0] // 2
    far = [pull(line, False, d) for d in (1, -1)]
    first = swap(line)
    if ready is not None:
        far, first, ready = after((far, first, ready))
    last = [pull(far[0][:half], False, 1), pull(far[1][half:], False, -1)]
    arrays = [line] + far + last
    return arrays + [first] + [swap(v) for v in far + last], ready


def send(value, distance):
    count = lax.axis_size("col")
    return lax.ppermute(value, "col", [(i, (i + distance) % count) for i in range(count)])


def sum_columns(near, own):
    half = own.shape[0] // 2
    far_up = send(near[4][:half], 2)
    far_down = send(near[4][half:], -2)
    up = send(near[3], 1)
    down = send(near[5], -1)
    next_up = send(near[1], 1)
    next_down = send(near[7], -1)
    f32 = jnp.float32
    relay_up = near[2].astype(f32) + up.astype(f32)
    relay_up = jnp.concatenate([relay_up[:half] + far_up.astype(f32), relay_up[half:]], axis=0)
    relay_down = near[6].astype(f32) + down.astype(f32)
    relay_down = jnp.concatenate(
        [relay_down[:half], relay_down[half:] + far_down.astype(f32)], axis=0
    )
    last_up = send(relay_up.astype(jnp.bfloat16), 2)
    last_down = send(relay_down.astype(jnp.bfloat16), -2)
    return [own, next_up, next_down, last_up, last_down]


def local(
    features,
    tile_values,
    slot_refs,
    wanted,
    time_ids,
    cond_ids,
    time_table,
    cond_table,
    gains,
    w_in,
    w_out,
):
    tile = tile_values.shape[-1]
    slots = tile_values.shape[3]
    row_tiles = tile_values.shape[0]
    matrix = tile_values.reshape(row_tiles, tile, slots * tile)
    slot_index = slot_refs.reshape(-1)
    wanted = wanted.reshape(-1)
    row = lax.axis_index("row")
    here = jnp.stack([row // (2 * SIDE), row // 2 % SIDE, row % 2, lax.axis_index("col")])
    scale_rows = gains[:, None, :] * (1.0 + lookup(cond_ids, cond_table))[None]
    shift_rows = lookup(time_ids, time_table).astype(jnp.bfloat16)
    piece = features.shape[1] // PIECES
    states = [features[:, p * piece : (p + 1) * piece] for p in range(PIECES)]
    ready = (matrix, wanted, slot_index, here)
    for layer in range(LAYERS):
        arrays, ready = gather_blocks(states[0], ready)
        if ready is not None:
            matrix, wanted, slot_index, here = ready
            ready = None
        near = {}
        for group in SENT:
            products = aggregate_tiles(matrix, arrays, here, wanted, slot_index, group)
            near.update(zip(group, products, strict=True))
        parts = [sum_columns(near, near[0])]
        last = layer == LAYERS - 1
        states = node_mlp(
            layer,
            states,
            parts,
            scale_rows,
            shift_rows,
            w_in,
            w_out,
            1 if last else PIECES,
        )
    return states[0]


def solution(mesh):
    return jax.shard_map(
        local,
        mesh=mesh,
        in_specs=(
            P(("row", "col"), None),
            P("row", "col", None, None, None),
            P("row", "col", None),
            P("row", "col", None, None),
            P(("row", "col")),
            P(("row", "col")),
            P(),
            P(),
            P(),
            P(),
            P(),
        ),
        out_specs=P(("row", "col"), None),
        check_vma=False,
    )
```

```python
import jax
import jax.numpy as jnp
from jax import lax
from jax.experimental import pallas as pl
from jax.experimental.pallas import tpu as pltpu
from jax.sharding import PartitionSpec as P

LAYERS = 2
PIECES = 1
VMEM_LIMIT = 20 * 1024 * 1024

epsilon = 1e-06


def lookup(ids, table):
    onehot = (ids[:, None] == jnp.arange(table.shape[0], dtype=jnp.int32)[None, :]).astype(
        jnp.bfloat16
    )
    return jnp.dot(onehot, table, preferred_element_type=jnp.float32)


def aggregate_tiles(matrix, sources, here, wanted, slot_index, further):
    row_tiles, tile, depth = matrix.shape
    slots = depth // tile
    width = sources[0].shape[-1]
    count = lax.axis_size("col")
    per_block = row_tiles // count
    n_src = len(sources)
    rows = per_block * tile

    def body(here_ref, wanted_ref, index_ref, matrix_ref, *refs):
        src = refs[:n_src]
        outs = refs[n_src:-1]
        tiles = refs[-1]
        x, y, core, col = (here_ref[i] for i in range(4))
        for array, block, first, second, swapped in BLOCKS:
            held = core ^ swapped
            step_x = jnp.where(held == 0, first, second)
            step_y = jnp.where(held == 0, second, first)
            p = place(x + step_x + SIDE, y + step_y + SIDE, held)
            start = pl.multiple_of(block * rows + wanted_ref[p] * tile, tile)
            tiles[p] = src[array][pl.ds(start, tile), :]
        for out, k in zip(outs, further, strict=True):
            for j in range(per_block):
                t = (col + k) % count * per_block + j
                right = jnp.concatenate(
                    [tiles[index_ref[t * slots + s]] for s in range(slots)], axis=0
                )
                value = jnp.dot(matrix_ref[t], right, preferred_element_type=jnp.float32)
                out[j * tile : (j + 1) * tile, :] = value.astype(jnp.bfloat16)

    smem = pl.BlockSpec(memory_space=pltpu.SMEM)
    vmem = pl.BlockSpec(memory_space=pltpu.VMEM)
    return pl.pallas_call(
        body,
        in_specs=[smem] * 3 + [vmem] * (1 + n_src),
        out_specs=[vmem] * len(further),
        out_shape=[jax.ShapeDtypeStruct((rows, width), jnp.bfloat16)] * len(further),
        scratch_shapes=[pltpu.VMEM((len(BLOCKS), tile, width), jnp.bfloat16)],
        compiler_params=pltpu.CompilerParams(vmem_limit_bytes=VMEM_LIMIT),
        name="aggregate_tiles",
    )(here, wanted, slot_index, matrix, *sources)


def node_mlp(layer, states, parts, scale_rows, shift_rows, w_in, w_out, pieces):
    rows = states[0].shape[0]
    width = w_out.shape[-1]
    hidden_units = w_in.shape[-1]
    chunks = 4
    chunk = hidden_units // chunks
    given = [[state, *addends] for state, addends in zip(states, parts, strict=True)]
    flat = [value for group in given for value in group]

    def body(scale_ref, shift_ref, w_in_ref, w_out_ref, *refs):
        inputs, outs = list(refs[: len(flat)]), refs[len(flat) :]
        sums = []
        for group in given:
            total = inputs.pop(0)[...].astype(jnp.float32)
            for _ in group[1:]:
                total = total + inputs.pop(0)[...].astype(jnp.float32)
            sums.append(total)
        pre = jnp.concatenate(sums, axis=1)
        scale = lax.rsqrt(jnp.mean(pre * pre, axis=-1, keepdims=True) + epsilon)
        normed = (
            pre * scale * scale_ref[layer] + shift_ref[...].astype(jnp.float32)
        ).astype(jnp.bfloat16)
        total = pre
        for k in range(chunks):
            units = pl.ds(k * chunk, chunk)
            inner = jnp.dot(
                normed, w_in_ref[layer, :, units], preferred_element_type=jnp.float32
            )
            hidden = (0.5 * inner * (1.0 + jnp.tanh(0.5 * inner))).astype(jnp.bfloat16)
            total = total + jnp.dot(
                hidden, w_out_ref[layer, units, :], preferred_element_type=jnp.float32
            )
        piece = width // pieces
        for p in range(pieces):
            outs[p][...] = total[:, p * piece : (p + 1) * piece].astype(jnp.bfloat16)

    vmem = pl.BlockSpec(memory_space=pltpu.VMEM)
    return pl.pallas_call(
        body,
        in_specs=[vmem] * (4 + len(flat)),
        out_specs=[vmem] * pieces,
        out_shape=[jax.ShapeDtypeStruct((rows, width // pieces), jnp.bfloat16)] * pieces,
        compiler_params=pltpu.CompilerParams(vmem_limit_bytes=VMEM_LIMIT),
        name="node_mlp",
    )(scale_rows, shift_rows, w_in, w_out, *flat)


SIDE = 4
NEAR = (2, 1, -1)


def held_blocks():
    line = (0, *NEAR)
    offsets = [[(e, d) for e in line] for d in (0, 1, -1)]
    offsets += [[(e, 2) for e in line[:2]], [(e, 2) for e in line[2:]]]
    count = len(offsets)
    return [
        (a + swapped * count, k, e, d, swapped)
        for swapped in (0, 1)
        for a, held in enumerate(offsets)
        for k, (e, d) in enumerate(held)
    ]


BLOCKS = held_blocks()
SENT = ((3, 5, 4), (2, 6, 1, 7, 0))


def place(x, y, core):
    return ((x % SIDE) * SIDE + y % SIDE) * 2 + core


def pull(value, first, distance):
    pairs = []
    for x in range(SIDE):
        for y in range(SIDE):
            for core in range(2):
                step = (distance, 0) if (core == 0) == first else (0, distance)
                pairs.append((place(x + step[0], y + step[1], core), place(x, y, core)))
    return lax.ppermute(value, "row", pairs)


def swap(value):
    count = 2 * SIDE * SIDE
    return lax.ppermute(value, "row", [(i, i ^ 1) for i in range(count)])


def gather_blocks(own, ready):
    after = lax.optimization_barrier
    line = jnp.concatenate([own] + [pull(own, True, e) for e in NEAR], axis=0)
    half = line.shape[0] // 2
    far = [pull(line, False, d) for d in (1, -1)]
    first = swap(line)
    if ready is not None:
        far, first, ready = after((far, first, ready))
    last = [pull(far[0][:half], False, 1), pull(far[1][half:], False, -1)]
    arrays = [line] + far + last
    return arrays + [first] + [swap(v) for v in far + last], ready


def send(value, distance):
    count = lax.axis_size("col")
    return lax.ppermute(value, "col", [(i, (i + distance) % count) for i in range(count)])


def sum_columns(near, own):
    half = own.shape[0] // 2
    far_up = send(near[4][:half], 2)
    far_down = send(near[4][half:], -2)
    up = send(near[3], 1)
    down = send(near[5], -1)
    next_up = send(near[1], 1)
    next_down = send(near[7], -1)
    f32 = jnp.float32
    relay_up = near[2].astype(f32) + up.astype(f32)
    relay_up = jnp.concatenate([relay_up[:half] + far_up.astype(f32), relay_up[half:]], axis=0)
    relay_down = near[6].astype(f32) + down.astype(f32)
    relay_down = jnp.concatenate(
        [relay_down[:half], relay_down[half:] + far_down.astype(f32)], axis=0
    )
    last_up = send(relay_up.astype(jnp.bfloat16), 2)
    last_down = send(relay_down.astype(jnp.bfloat16), -2)
    return [own, next_up, next_down, last_up, last_down]


def local(
    features,
    tile_values,
    slot_refs,
    wanted,
    time_ids,
    cond_ids,
    time_table,
    cond_table,
    gains,
    w_in,
    w_out,
):
    tile = tile_values.shape[-1]
    slots = tile_values.shape[3]
    row_tiles = tile_values.shape[0]
    matrix = tile_values.reshape(row_tiles, tile, slots * tile)
    slot_index = slot_refs.reshape(-1)
    wanted = wanted.reshape(-1)
    row = lax.axis_index("row")
    here = jnp.stack([row // (2 * SIDE), row // 2 % SIDE, row % 2, lax.axis_index("col")])
    scale_rows = gains[:, None, :] * (1.0 + lookup(cond_ids, cond_table))[None]
    shift_rows = lookup(time_ids, time_table).astype(jnp.bfloat16)
    piece = features.shape[1] // PIECES
    states = [features[:, p * piece : (p + 1) * piece] for p in range(PIECES)]
    ready = (matrix, wanted, slot_index, here)
    for layer in range(LAYERS):
        arrays, ready = gather_blocks(states[0], ready)
        if ready is not None:
            matrix, wanted, slot_index, here = ready
            ready = None
        near = {}
        for group in SENT:
            products = aggregate_tiles(matrix, arrays, here, wanted, slot_index, group)
            near.update(zip(group, products, strict=True))
        parts = [sum_columns(near, near[0])]
        last = layer == LAYERS - 1
        states = node_mlp(
            layer,
            states,
            parts,
            scale_rows,
            shift_rows,
            w_in,
            w_out,
            1 if last else PIECES,
        )
    return states[0]


def solution(mesh):
    return jax.shard_map(
        local,
        mesh=mesh,
        in_specs=(
            P(("row", "col"), None),
            P("row", "col", None, None, None),
            P("row", "col", None),
            P("row", "col", None, None),
            P(("row", "col")),
            P(("row", "col")),
            P(),
            P(),
            P(),
            P(),
            P(),
        ),
        out_specs=P(("row", "col"), None),
        check_vma=False,
    )
```

```python
import jax
import jax.numpy as jnp
from jax import lax
from jax.experimental import pallas as pl
from jax.experimental.pallas import tpu as pltpu
from jax.sharding import PartitionSpec as P

LAYERS = 2
PIECES = 1
VMEM_LIMIT = 20 * 1024 * 1024

epsilon = 1e-06


def lookup(ids, table):
    onehot = (ids[:, None] == jnp.arange(table.shape[0], dtype=jnp.int32)[None, :]).astype(
        jnp.bfloat16
    )
    return jnp.dot(onehot, table, preferred_element_type=jnp.float32)


def aggregate_tiles(matrix, sources, here, wanted, slot_index, further):
    return multiply_tiles(matrix, sources, here, wanted, slot_index, further, True)


def multiply_tiles(matrix, sources, here, wanted, slot_index, further, gather):
    row_tiles, tile, depth = matrix.shape
    slots = depth // tile
    width = sources[0].shape[-1]
    n_out = len(further)
    count = lax.axis_size("col")
    per_block = row_tiles // count
    n_src = len(sources)
    rows = per_block * tile

    def body(here_ref, wanted_ref, index_ref, matrix_ref, *refs):
        src = refs[:n_src]
        outs = refs[n_src : n_src + n_out]
        tiles = refs[-1] if gather else src[0]
        x, y, core, col = (here_ref[i] for i in range(4))
        for array, block, first, second, swapped in BLOCKS if gather else ():
            held = core ^ swapped
            step_x = jnp.where(held == 0, first, second)
            step_y = jnp.where(held == 0, second, first)
            p = place(x + step_x + SIDE, y + step_y + SIDE, held)
            start = pl.multiple_of(block * rows + wanted_ref[p] * tile, tile)
            tiles[p] = src[array][pl.ds(start, tile), :]
        for out, k in zip(outs, further, strict=True):
            for j in range(per_block):
                t = (col + k) % count * per_block + j
                right = jnp.concatenate(
                    [tiles[index_ref[t * slots + s]] for s in range(slots)], axis=0
                )
                value = jnp.dot(matrix_ref[t], right, preferred_element_type=jnp.float32)
                out[j * tile : (j + 1) * tile, :] = value.astype(jnp.bfloat16)

    smem = pl.BlockSpec(memory_space=pltpu.SMEM)
    vmem = pl.BlockSpec(memory_space=pltpu.VMEM)
    return pl.pallas_call(
        body,
        in_specs=[smem] * 3 + [vmem] * (1 + n_src),
        out_specs=[vmem] * (n_out + gather),
        out_shape=[jax.ShapeDtypeStruct((rows, width), jnp.bfloat16)] * n_out
        + [jax.ShapeDtypeStruct((len(BLOCKS), tile, width), jnp.bfloat16)] * gather,
        compiler_params=pltpu.CompilerParams(vmem_limit_bytes=VMEM_LIMIT),
        name="aggregate_tiles",
    )(here, wanted, slot_index, matrix, *sources)


def node_mlp(layer, states, parts, scale_rows, shift_rows, w_in, w_out, pieces):
    rows = states[0].shape[0]
    width = w_out.shape[-1]
    hidden_units = w_in.shape[-1]
    chunks = 4
    chunk = hidden_units // chunks
    given = [[state, *addends] for state, addends in zip(states, parts, strict=True)]
    flat = [value for group in given for value in group]

    def body(scale_ref, shift_ref, w_in_ref, w_out_ref, *refs):
        inputs, outs = list(refs[: len(flat)]), refs[len(flat) :]
        sums = []
        for group in given:
            total = inputs.pop(0)[...].astype(jnp.float32)
            for _ in group[1:]:
                total = total + inputs.pop(0)[...].astype(jnp.float32)
            sums.append(total)
        pre = jnp.concatenate(sums, axis=1)
        scale = lax.rsqrt(jnp.mean(pre * pre, axis=-1, keepdims=True) + epsilon)
        normed = (
            pre * scale * scale_ref[layer] + shift_ref[...].astype(jnp.float32)
        ).astype(jnp.bfloat16)
        total = pre
        for k in range(chunks):
            units = pl.ds(k * chunk, chunk)
            inner = jnp.dot(
                normed, w_in_ref[layer, :, units], preferred_element_type=jnp.float32
            )
            hidden = (0.5 * inner * (1.0 + jnp.tanh(0.5 * inner))).astype(jnp.bfloat16)
            total = total + jnp.dot(
                hidden, w_out_ref[layer, units, :], preferred_element_type=jnp.float32
            )
        piece = width // pieces
        for p in range(pieces):
            outs[p][...] = total[:, p * piece : (p + 1) * piece].astype(jnp.bfloat16)

    vmem = pl.BlockSpec(memory_space=pltpu.VMEM)
    return pl.pallas_call(
        body,
        in_specs=[vmem] * (4 + len(flat)),
        out_specs=[vmem] * pieces,
        out_shape=[jax.ShapeDtypeStruct((rows, width // pieces), jnp.bfloat16)] * pieces,
        compiler_params=pltpu.CompilerParams(vmem_limit_bytes=VMEM_LIMIT),
        name="node_mlp",
    )(scale_rows, shift_rows, w_in, w_out, *flat)


SIDE = 4
NEAR = (2, 1, -1)


def held_blocks():
    line = (0, *NEAR)
    offsets = [[(e, d) for e in line] for d in (0, 1, -1)]
    offsets += [[(e, 2) for e in line[:2]], [(e, 2) for e in line[2:]]]
    count = len(offsets)
    return [
        (a + swapped * count, k, e, d, swapped)
        for swapped in (0, 1)
        for a, held in enumerate(offsets)
        for k, (e, d) in enumerate(held)
    ]


BLOCKS = held_blocks()
SENT = ((3, 5, 4), (2, 6, 1, 7, 0))


def place(x, y, core):
    return ((x % SIDE) * SIDE + y % SIDE) * 2 + core


def pull(value, first, distance):
    pairs = []
    for x in range(SIDE):
        for y in range(SIDE):
            for core in range(2):
                step = (distance, 0) if (core == 0) == first else (0, distance)
                pairs.append((place(x + step[0], y + step[1], core), place(x, y, core)))
    return lax.ppermute(value, "row", pairs)


def swap(value):
    count = 2 * SIDE * SIDE
    return lax.ppermute(value, "row", [(i, i ^ 1) for i in range(count)])


def gather_blocks(own, ready):
    after = lax.optimization_barrier
    line = jnp.concatenate([own] + [pull(own, True, e) for e in NEAR], axis=0)
    half = line.shape[0] // 2
    far = [pull(line, False, d) for d in (1, -1)]
    first = swap(line)
    if ready is not None:
        far, first, ready = after((far, first, ready))
    last = [pull(far[0][:half], False, 1), pull(far[1][half:], False, -1)]
    arrays = [line] + far + last
    return arrays + [first] + [swap(v) for v in far + last], ready


def send(value, distance):
    count = lax.axis_size("col")
    return lax.ppermute(value, "col", [(i, (i + distance) % count) for i in range(count)])


def sum_columns(near, own):
    half = own.shape[0] // 2
    far_up = send(near[4][:half], 2)
    far_down = send(near[4][half:], -2)
    up = send(near[3], 1)
    down = send(near[5], -1)
    next_up = send(near[1], 1)
    next_down = send(near[7], -1)
    f32 = jnp.float32
    relay_up = near[2].astype(f32) + up.astype(f32)
    relay_up = jnp.concatenate([relay_up[:half] + far_up.astype(f32), relay_up[half:]], axis=0)
    relay_down = near[6].astype(f32) + down.astype(f32)
    relay_down = jnp.concatenate(
        [relay_down[:half], relay_down[half:] + far_down.astype(f32)], axis=0
    )
    last_up = send(relay_up.astype(jnp.bfloat16), 2)
    last_down = send(relay_down.astype(jnp.bfloat16), -2)
    return [own, next_up, next_down, last_up, last_down]


def local(
    features,
    tile_values,
    slot_refs,
    wanted,
    time_ids,
    cond_ids,
    time_table,
    cond_table,
    gains,
    w_in,
    w_out,
):
    tile = tile_values.shape[-1]
    slots = tile_values.shape[3]
    row_tiles = tile_values.shape[0]
    matrix = tile_values.reshape(row_tiles, tile, slots * tile)
    slot_index = slot_refs.reshape(-1)
    wanted = wanted.reshape(-1)
    row = lax.axis_index("row")
    here = jnp.stack([row // (2 * SIDE), row // 2 % SIDE, row % 2, lax.axis_index("col")])
    scale_rows = gains[:, None, :] * (1.0 + lookup(cond_ids, cond_table))[None]
    shift_rows = lookup(time_ids, time_table).astype(jnp.bfloat16)
    piece = features.shape[1] // PIECES
    states = [features[:, p * piece : (p + 1) * piece] for p in range(PIECES)]
    ready = (matrix, wanted, slot_index, here)
    for layer in range(LAYERS):
        arrays, ready = gather_blocks(states[0], ready)
        if ready is not None:
            matrix, wanted, slot_index, here = ready
            ready = None
        near = {}
        *products, tiles = aggregate_tiles(matrix, arrays, here, wanted, slot_index, SENT[0])
        near.update(zip(SENT[0], products, strict=True))
        products = multiply_tiles(matrix, [tiles], here, wanted, slot_index, SENT[1], False)
        near.update(zip(SENT[1], products, strict=True))
        parts = [sum_columns(near, near[0])]
        last = layer == LAYERS - 1
        states = node_mlp(
            layer,
            states,
            parts,
            scale_rows,
            shift_rows,
            w_in,
            w_out,
            1 if last else PIECES,
        )
    return states[0]


def solution(mesh):
    return jax.shard_map(
        local,
        mesh=mesh,
        in_specs=(
            P(("row", "col"), None),
            P("row", "col", None, None, None),
            P("row", "col", None),
            P("row", "col", None, None),
            P(("row", "col")),
            P(("row", "col")),
            P(),
            P(),
            P(),
            P(),
            P(),
        ),
        out_specs=P(("row", "col"), None),
        check_vma=False,
    )
```
